512 devices in a mesh: row: 16 (over z_lo, y), mode: 32 (over z_hi, x, core).
Axes of the slice: x: 4, y: 4, z: 16 (z_hi: 4, z_lo: 4; z = z_hi * 4 + z_lo), core: 2. Of those that a mesh axis runs over, the one named last changes fastest.
Arguments:
- transfer_matrix: float32 [2, 3072, 49152], P(None, 'row', 'mode'), may hold values from -0.01953125 to 0.01953125
- probes: float32 [2, 49152, 256], P(None, ('mode', 'row')), may hold values from -6 to 6
- intensity: float32 [3072, 256], P('row'), may hold values from 0.25 to 4
Outputs:
- gradient: float32 [2, 3072, 49152], P(None, 'row', 'mode')
The draws below stay inside these ranges and needn't reach their ends.
All inputs are finite; a program needn't handle non-finite values.
Results may differ from the reference program's by a relative error of at most 0.00012.
Values sent between devices are 32-bit elements; how exact they have to be, the bound alone decides.
A program may use at most 64 MiB of HBM per device.

```python
import math
import jax
import jax.numpy as jnp
from jax import lax

N = 49152
P_SIZE = 256
M = 3072


def block_levels(own_key, extent, cuts, low, high):
    loudness = 1.0
    for dim, blocks in cuts:
        draws = jax.random.uniform(jax.random.fold_in(jax.random.fold_in(own_key, 6), dim), (blocks,), jnp.float32, low / len(cuts), high / len(cuts))
        loudness = loudness * jnp.repeat(jnp.exp(draws), extent[dim] // blocks).reshape((-1,) + (1,) * (len(extent) - 1 - dim))
    return loudness


def centred(rng, shape, scale, limit, split=(), held_as=jnp.bfloat16):
    values = scale * jax.random.normal(rng, shape, jnp.float32)
    if split:
        values = values * block_levels(rng, shape, split, -0.22, 0.18)
    return jnp.clip(values, -limit, limit).astype(held_as)


def setup_inputs(seed: int = 0) -> dict:
    streams_of = jax.random.split(jax.random.key(seed), 4)
    transfer_matrix = centred(streams_of[0], (2, M, N), (2 * N) ** -0.5, 0.01953125, ((1, 16), (2, 32)), jnp.float32)
    probes = centred(streams_of[1], (2, N, P_SIZE), 1.0, 6.0, ((1, 512),), jnp.float32)
    intensity = jnp.clip(jnp.exp(math.log(4.0) - 2.7725887 * jax.random.uniform(streams_of[2], (M, P_SIZE), jnp.float32) ** block_levels(streams_of[2], (M, P_SIZE), ((0, 16),), -0.2, 0.2)), 0.25, 4.0)
    return dict(transfer_matrix=transfer_matrix, probes=probes, intensity=intensity)


def exact_dot(left, right):
    return jnp.dot(left, right, precision=lax.Precision.HIGHEST, preferred_element_type=jnp.float32)


def exact_dot_transposed(left, right):
    return lax.dot_general(left, right, (((1,), (1,)), ((), ())), precision=lax.Precision.HIGHEST, preferred_element_type=jnp.float32)


def reference(transfer_matrix, probes, intensity):
    fields_real = exact_dot(transfer_matrix[0], probes[0]) - exact_dot(transfer_matrix[1], probes[1])
    fields_imag = exact_dot(transfer_matrix[0], probes[1]) + exact_dot(transfer_matrix[1], probes[0])
    excess = fields_real * fields_real + fields_imag * fields_imag - intensity
    resid_real = excess * fields_real / P_SIZE
    resid_imag = excess * fields_imag / P_SIZE
    grad_real = exact_dot_transposed(resid_real, probes[0]) + exact_dot_transposed(resid_imag, probes[1])
    grad_imag = exact_dot_transposed(resid_imag, probes[0]) - exact_dot_transposed(resid_real, probes[1])
    return jnp.stack([grad_real, grad_imag])
```

```python
import jax
import jax.numpy as jnp
from jax import lax
from jax.experimental import pallas as pl
from jax.experimental.pallas import tpu as pltpu
from jax.sharding import Mesh
from jax.sharding import PartitionSpec as P

AXES = ("zl", "y", "zh", "x", "c")
SIZES = {"zl": 4, "y": 4, "zh": 4, "x": 4, "c": 2}
CHUNKS = ((0, 128), (128, 64), (192, 64))
BY_MESH = pl.DeviceIdType.MESH
XC = tuple((dx, dc) for dx in range(4) for dc in range(2) if (dx, dc) != (0, 0))
F32, BF16 = jnp.float32, jnp.bfloat16


def shifted(axis, by):
    return lax.rem(lax.axis_index(axis) + by, SIZES[axis])


def partner(index, j):
    if j == 0:
        return index
    if j == 1:
        return index + 1 - 2 * lax.rem(index, 2)
    if j == 2:
        return lax.rem(index + 2, 4)
    return 3 - index


def halves(value):
    high = value.astype(BF16)
    return high, (value - high.astype(F32)).astype(BF16)


def dot3(a_high, a_low, b_high, b_low, contract_b):
    dims = (((1,), (contract_b,)), ((), ()))

    def dot(a, b):
        return lax.dot_general(a, b, dims, preferred_element_type=F32)

    return dot(a_high, b_high) + (dot(a_high, b_low) + dot(a_low, b_high))


def swapped(value, signs):
    width = value.shape[1] // 2
    if width % 128 == 0:
        turned = jnp.concatenate([value[:, width:], value[:, :width]], axis=1)
    else:
        turned = pltpu.roll(value, width, 1)
    return turned * signs


def sign_row(width, first, second):
    lane = lax.broadcasted_iota(jnp.int32, (1, 2 * width), 1)
    return jnp.where(lane < width, F32(first), F32(second))


def gather_kernel(
    u_hbm, s_ref, i_ref, *rest
):
    n = len(CHUNKS)
    grad, res_h, res_l, last_h, last_l = rest[:5]
    uf, uh, ul, u_sem = rest[5:9]
    per = [rest[9 + 14 * k : 9 + 14 * (k + 1)] for k in range(n)]
    zl, y, x, c = (lax.axis_index(a) for a in ("zl", "y", "x", "c"))
    own = x * 2 + c
    up, down = shifted("y", 1), shifted("y", 3)
    rows = i_ref.shape[0] // 8

    u_copy = pltpu.make_async_copy(u_hbm, uf, u_sem)
    u_copy.start()

    barrier = pltpu.get_barrier_semaphore()
    peers = [{"zl": partner(zl, j)} for j in (1, 2, 3)]
    peers += [{"y": up}, {"y": down}]
    peers += [{"x": shifted("x", dx), "c": shifted("c", dc)} for dx, dc in XC]
    peers += [{"zh": shifted("zh", d)} for d in (1, 2, 3)]
    for peer in peers:
        pl.semaphore_signal(barrier, inc=1, device_id=peer, device_id_type=BY_MESH)

    for k, (first, width) in enumerate(CHUNKS):
        strip = per[k][0]
        packed = jnp.concatenate(
            [s_ref[0, :, first : first + width], s_ref[1, :, first : first + width]], axis=1
        )
        strip[zl, y] = packed.reshape(2, 48, 2 * width)
        mine = i_ref[pl.ds(pl.multiple_of(own * rows, 8), rows), first : first + width]
        per[k][7][...] = jnp.concatenate([mine, mine], axis=1)

    pl.semaphore_wait(barrier, len(peers))

    sent = []

    def send(src, dst, send_sem, recv_sem, peer):
        copy = pltpu.make_async_remote_copy(
            src_ref=src, dst_ref=dst, send_sem=send_sem, recv_sem=recv_sem,
            device_id=peer, device_id_type=BY_MESH,
        )
        copy.start()
        sent.append(copy)
        return copy

    def issue(k):
        strip, zs, zr, ys, yr = per[k][0], *per[k][8:12]
        block = strip.at[zl, y]
        z = [
            send(block, block, zs.at[j - 1], zr.at[j - 1], {"zl": partner(zl, j)})
            for j in (1, 2, 3)
        ]
        return z, {0: both_ways(k, 0)}

    def both_ways(k, j):
        strip, ys, yr = per[k][0], per[k][10], per[k][11]
        block = strip.at[partner(zl, j), y]
        return (
            send(block, block, ys.at[j, 0], yr.at[j, 0], {"y": up}),
            send(block, block, ys.at[j, 1], yr.at[j, 1], {"y": down}),
        )

    def relay(k, j, arrivals):
        strip, ys, yr = per[k][0], per[k][10], per[k][11]
        g = partner(zl, j)
        arrivals[0].wait_recv()
        from_down = strip.at[g, down, 0]
        a = send(from_down, from_down, ys.at[j, 2], yr.at[j, 2], {"y": up})
        arrivals[1].wait_recv()
        from_up = strip.at[g, up, 1]
        b = send(from_up, from_up, ys.at[j, 3], yr.at[j, 3], {"y": down})
        return a, b

    def gather(k, started):
        z, y_copies = started
        far = {}
        for j in (0, 1, 2, 3):
            if j < 3:
                z[j].wait_recv()
                y_copies[j + 1] = both_ways(k, j + 1)
            far[j] = relay(k, j, y_copies[j])
        return far

    def fields(k, far):
        strip, sh, sl, total = per[k][:4]
        width = CHUNKS[k][1]
        for j in (0, 1, 2, 3):
            for copy in far[j]:
                copy.wait_recv()
            g = partner(zl, j)
            high, low = halves(strip[g].reshape(384, 2 * width))
            sh[g] = high
            sl[g] = low
            value = dot3(uh[g], ul[g], high, low, 0)
            if j == 0:
                total[...] = value
            else:
                total[...] += value

    def spread_fields(k):
        total, parts, got = per[k][3:6]
        width = CHUNKS[k][1]
        half = total.shape[0] // 2
        value = total[:half, :] + swapped(total[half:, :], sign_row(width, -1, 1))
        parts[...] = value.reshape(parts.shape)
        xs, xr = per[k][12].at[0], per[k][13].at[0]
        copies = []
        for i, (dx, dc) in enumerate(XC):
            tx, tc = shifted("x", dx), shifted("c", dc)
            copies.append(
                send(parts.at[tx * 2 + tc], got.at[i], xs.at[i], xr.at[i], {"x": tx, "c": tc})
            )
        return copies

    def sum_over_x(k, copies):
        parts, got, share = per[k][4], per[k][5], per[k][6]
        for copy in copies:
            copy.wait_recv()
        value = parts[own]
        for i in range(7):
            value = value + got[i]
        share[0] = value
        xs, xr = per[k][12].at[1], per[k][13].at[1]
        return [
            send(share.at[0], share.at[d], xs.at[d], xr.at[d], {"zh": shifted("zh", d)})
            for d in (1, 2, 3)
        ]

    def spread_residual(k, copies):
        parts, share, measured = per[k][4], per[k][6], per[k][7]
        got = per[k][5]
        width = CHUNKS[k][1]
        for copy in copies:
            copy.wait_recv()
        value = (share[0] + share[1]) + (share[2] + share[3])
        square = value * value
        excess = square + swapped(square, F32(1)) - measured[...]
        share[4] = excess * value * F32(1 / 256)
        gathered = per[k][3]
        place = gathered.at[pl.ds(pl.multiple_of(own * rows, 8), rows), :]
        xs, xr = per[k][12].at[2], per[k][13].at[2]
        out = []
        for i, (dx, dc) in enumerate(XC):
            peer = {"x": shifted("x", dx), "c": shifted("c", dc)}
            out.append(send(share.at[4], place, xs.at[i], xr.at[i], peer))
        gathered[pl.ds(pl.multiple_of(own * rows, 8), rows), :] = share[4]
        return out

    def residual_rows(k, copies):
        width = CHUNKS[k][1]
        for copy in copies:
            copy.wait_recv()
        value = per[k][3][: 8 * rows, :]
        stacked = jnp.concatenate([value, swapped(value, sign_row(width, 1, -1))], axis=0)
        return halves(stacked)

    def gradient(k, copies, add):
        high, low = residual_rows(k, copies)
        sh, sl = per[k][1], per[k][2]
        for g in range(4):
            value = dot3(high, low, sh[g], sl[g], 1).reshape(2, 8 * rows, 384)
            if add:
                grad[:, :, g * 384 : (g + 1) * 384] += value
            else:
                grad[:, :, g * 384 : (g + 1) * 384] = value

    started = [issue(k) for k in range(n)]

    u_copy.wait()
    for g in range(4):
        for p in range(2):
            high, low = halves(uf[p, :, g * 384 : (g + 1) * 384])
            uh[g, p * 192 : (p + 1) * 192, :] = high
            ul[g, p * 192 : (p + 1) * 192, :] = low

    fields(0, gather(0, started[0]))
    x0 = spread_fields(0)
    far1 = gather(1, started[1])
    z0 = sum_over_x(0, x0)
    fields(1, far1)
    x1 = spread_fields(1)
    far2 = gather(2, started[2])
    r0 = spread_residual(0, z0)
    z1 = sum_over_x(1, x1)
    fields(2, far2)
    x2 = spread_fields(2)
    gradient(0, r0, False)
    z2 = sum_over_x(2, x2)
    r1 = spread_residual(1, z1)
    gradient(1, r1, True)
    r2 = spread_residual(2, z2)
    last_h[...] = per[n - 1][1][...]
    last_l[...] = per[n - 1][2][...]
    high, low = residual_rows(2, r2)
    res_h[...] = high
    res_l[...] = low
    for copy in sent:
        copy.wait_send()


def finish_kernel(grad, res_h, res_l, last_h, last_l, out, done, sems):
    copies = []
    for g in range(4):
        value = dot3(res_h[...], res_l[...], last_h[g], last_l[g], 1)
        columns = pl.ds(g * 384, 384)
        done[:, :, columns] = grad[:, :, columns] + value.reshape(2, value.shape[0] // 2, 384)
        copy = pltpu.make_async_copy(done.at[:, :, columns], out.at[:, :, columns], sems.at[g])
        copy.start()
        copies.append(copy)
    for copy in copies:
        copy.wait()


def body(transfer_matrix, probes, intensity):
    _, m, cols = transfer_matrix.shape
    rows = m // 8
    width = CHUNKS[-1][1]
    vmem = pl.BlockSpec(memory_space=pltpu.VMEM)
    hbm = pl.BlockSpec(memory_space=pltpu.HBM)
    scratch = [
        pltpu.VMEM((2, m, cols), F32),
        pltpu.VMEM((4, 2 * m, cols // 4), BF16),
        pltpu.VMEM((4, 2 * m, cols // 4), BF16),
        pltpu.SemaphoreType.DMA,
    ]
    for _, w in CHUNKS:
        scratch += [
            pltpu.VMEM((4, 4, 2, 48, 2 * w), F32),
            pltpu.VMEM((4, cols // 4, 2 * w), BF16),
            pltpu.VMEM((4, cols // 4, 2 * w), BF16),
            pltpu.VMEM((2 * m, 2 * w), F32),
            pltpu.VMEM((8, rows, 2 * w), F32),
            pltpu.VMEM((7, rows, 2 * w), F32),
            pltpu.VMEM((5, rows, 2 * w), F32),
            pltpu.VMEM((rows, 2 * w), F32),
            pltpu.SemaphoreType.DMA((3,)),
            pltpu.SemaphoreType.DMA((3,)),
            pltpu.SemaphoreType.DMA((4, 4)),
            pltpu.SemaphoreType.DMA((4, 4)),
            pltpu.SemaphoreType.DMA((3, 7)),
            pltpu.SemaphoreType.DMA((3, 7)),
        ]
    outs = pl.pallas_call(
        gather_kernel,
        out_shape=(
            jax.ShapeDtypeStruct((2, m, cols), F32),
            jax.ShapeDtypeStruct((2 * m, 2 * width), BF16),
            jax.ShapeDtypeStruct((2 * m, 2 * width), BF16),
            jax.ShapeDtypeStruct((4, cols // 4, 2 * width), BF16),
            jax.ShapeDtypeStruct((4, cols // 4, 2 * width), BF16),
        ),
        in_specs=[hbm, vmem, vmem],
        out_specs=(vmem,) * 5,
        scratch_shapes=scratch,
        compiler_params=pltpu.CompilerParams(
            collective_id=0, has_side_effects=True, vmem_limit_bytes=32 * 1024 * 1024
        ),
        name="gather",
    )(transfer_matrix, probes, intensity)
    return pl.pallas_call(
        finish_kernel,
        out_shape=jax.ShapeDtypeStruct((2, m, cols), F32),
        in_specs=[vmem] * 5,
        out_specs=hbm,
        scratch_shapes=[pltpu.VMEM((2, m, cols), F32), pltpu.SemaphoreType.DMA((4,))],
        compiler_params=pltpu.CompilerParams(vmem_limit_bytes=32 * 1024 * 1024),
        name="finish",
    )(*outs)


def solution(mesh):
    split = Mesh(mesh.devices.reshape([SIZES[a] for a in AXES]), AXES)
    row, mode = ("zl", "y"), ("zh", "x", "c")
    placed = (P(None, row, mode), P(None, mode + row, None), P(row, None))
    return jax.shard_map(
        body, mesh=split, in_specs=placed, out_specs=P(None, row, mode), check_vma=False
    )
```

```python
import jax
import jax.numpy as jnp
from jax import lax
from jax.experimental import pallas as pl
from jax.experimental.pallas import tpu as pltpu
from jax.sharding import Mesh
from jax.sharding import PartitionSpec as P

AXES = ("zl", "y", "zh", "x", "c")
SIZES = {"zl": 4, "y": 4, "zh": 4, "x": 4, "c": 2}
CHUNKS = ((0, 128), (128, 64), (192, 64))
BY_MESH = pl.DeviceIdType.MESH
XC = tuple((dx, dc) for dx in range(4) for dc in range(2) if (dx, dc) != (0, 0))
F32, BF16 = jnp.float32, jnp.bfloat16


def shifted(axis, by):
    return lax.rem(lax.axis_index(axis) + by, SIZES[axis])


def along_z(by):
    z = lax.rem(lax.axis_index("zh") * 4 + lax.axis_index("zl") + (by + 16), 16)
    return {"zh": lax.div(z, 4), "zl": lax.rem(z, 4)}


def partner(index, j):
    if j == 0:
        return index
    if j == 1:
        return index + 1 - 2 * lax.rem(index, 2)
    if j == 2:
        return lax.rem(index + 2, 4)
    return 3 - index


def halves(value):
    high = value.astype(BF16)
    return high, (value - high.astype(F32)).astype(BF16)


def dot3(a_high, a_low, b_high, b_low, contract_b):
    dims = (((1,), (contract_b,)), ((), ()))

    def dot(a, b):
        return lax.dot_general(a, b, dims, preferred_element_type=F32)

    return dot(a_high, b_high) + (dot(a_high, b_low) + dot(a_low, b_high))


def swapped(value, signs):
    width = value.shape[1] // 2
    if width % 128 == 0:
        turned = jnp.concatenate([value[:, width:], value[:, :width]], axis=1)
    else:
        turned = pltpu.roll(value, width, 1)
    return turned * signs


def sign_row(width, first, second):
    lane = lax.broadcasted_iota(jnp.int32, (1, 2 * width), 1)
    return jnp.where(lane < width, F32(first), F32(second))


def stacked_residual(value):
    turned = swapped(value, sign_row(value.shape[1] // 2, 1, -1))
    return halves(jnp.concatenate([value, turned], axis=0))


def gather_kernel(u_hbm, s_hbm, i_hbm, *rest):
    n = len(CHUNKS)
    grad_out, res_out, last_h, last_l = rest[:4]
    uf, uh, ul, s_ref, i_ref, grad, in_sems, out_sems, near = rest[4:13]
    per = [rest[13 + 14 * k : 13 + 14 * (k + 1)] for k in range(n)]
    zl, y, x, c = (lax.axis_index(a) for a in ("zl", "y", "x", "c"))
    own = x * 2 + c
    up, down = shifted("y", 1), shifted("y", 3)
    rows = i_ref.shape[0]
    own_rows = pl.ds(pl.multiple_of(own * rows, 8), rows)

    s_copy = pltpu.make_async_copy(s_hbm, s_ref, in_sems.at[0])
    i_copy = pltpu.make_async_copy(i_hbm.at[own_rows, :], i_ref, in_sems.at[1])
    u_copy = pltpu.make_async_copy(u_hbm, uf, in_sems.at[2])
    s_copy.start()
    i_copy.start()
    u_copy.start()

    barrier = pltpu.get_barrier_semaphore()
    peers = [{"zl": partner(zl, j)} for j in (1, 2, 3)]
    peers += [{"y": up}, {"y": down}]
    peers += [{"x": shifted("x", dx), "c": shifted("c", dc)} for dx, dc in XC]
    peers += [along_z(1), along_z(-1)]
    for peer in peers:
        pl.semaphore_signal(barrier, inc=1, device_id=peer, device_id_type=BY_MESH)

    s_copy.wait()
    i_copy.wait()
    for k, (first, width) in enumerate(CHUNKS):
        strip = per[k][0]
        packed = jnp.concatenate(
            [s_ref[0, :, first : first + width], s_ref[1, :, first : first + width]], axis=1
        )
        strip[zl * 4 + y] = packed.reshape(2, 48, 2 * width)
        mine = i_ref[:, first : first + width]
        per[k][7][...] = jnp.concatenate([mine, mine], axis=1)

    pl.semaphore_wait(barrier, len(peers))

    def announce(i):
        for by in (1 << i, -(1 << i)):
            pl.semaphore_signal(near.at[i], inc=1, device_id=along_z(by), device_id_type=BY_MESH)

    def heard(i):
        pl.semaphore_wait(near.at[i], 2)

    announce(0)

    def send(src, dst, send_sem, recv_sem, peer):
        pltpu.make_async_remote_copy(
            src_ref=src, dst_ref=dst, send_sem=send_sem, recv_sem=recv_sem,
            device_id=peer, device_id_type=BY_MESH,
        ).start()

    def await_bytes(of, sem):
        pltpu.make_async_copy(of, of, sem).wait()

    def place(j, at):
        return partner(zl, j) * 4 + at

    def both_ways(k, j):
        strip, sem, arrived = per[k][0], per[k][8], per[k][10].at[j]
        block = strip.at[place(j, y)]
        send(block, block, sem, arrived, {"y": up})
        send(block, block, sem, arrived, {"y": down})
        if direct(k, j):
            send(block, block, sem, per[k][11].at[j], {"y": shifted("y", 2)})

    def direct(k, j):
        return k == n - 1 and j == 3

    def issue(k):
        strip, sem, arrived = per[k][0], per[k][8], per[k][9]
        block = strip.at[place(0, y)]
        for j in (1, 2, 3):
            send(block, block, sem, arrived.at[j - 1], {"zl": partner(zl, j)})
        both_ways(k, 0)

    def relay(k, j):
        strip, sem, arrived = per[k][0], per[k][8], per[k][11].at[j]
        await_bytes(strip.at[pl.ds(0, 2)], per[k][10].at[j])
        if not direct(k, j):
            from_down = strip.at[place(j, down), 0]
            from_up = strip.at[place(j, up), 1]
            send(from_down, from_down, sem, arrived, {"y": up})
            send(from_up, from_up, sem, arrived, {"y": down})

    def forward(k, j):
        await_bytes(per[k][0].at[0], per[k][9].at[j - 1])
        both_ways(k, j)

    def relay_all(k):
        for j in (0, 1, 2, 3):
            relay(k, j)

    def gather(k):
        for j in (0, 1, 2, 3):
            if j < 3:
                forward(k, j + 1)
                heard(j)
                if j < 2:
                    announce(j + 1)
            relay(k, j)

    def forward_all(k):
        for j in (1, 2, 3):
            forward(k, j)

    def fields(k):
        strip, sh, sl, total = per[k][:4]
        width = CHUNKS[k][1]
        for j in (0, 1, 2, 3):
            await_bytes(strip.at[0], per[k][11].at[j])
            g = partner(zl, j)
            value = strip[pl.ds(pl.multiple_of(g * 4, 4), 4)]
            high, low = halves(value.reshape(384, 2 * width))
            sh[g] = high
            sl[g] = low
            value = dot3(uh[g], ul[g], high, low, 0)
            if j == 0:
                total[...] = value
            else:
                total[...] += value

    def spread_fields(k):
        total, parts, got = per[k][3:6]
        width = CHUNKS[k][1]
        half = total.shape[0] // 2
        value = total[:half, :] + swapped(total[half:, :], sign_row(width, -1, 1))
        parts[...] = value.reshape(parts.shape)
        for i, (dx, dc) in enumerate(XC):
            tx, tc = shifted("x", dx), shifted("c", dc)
            part = parts.at[tx * 2 + tc]
            send(part, got.at[i], per[k][12].at[0], per[k][13].at[0], {"x": tx, "c": tc})

    def sum_over_x(k):
        parts, got, share = per[k][4], per[k][5], per[k][6]
        await_bytes(got, per[k][13].at[0])
        value = parts[own]
        for i in range(7):
            value = value + got[i]
        share[0] = value
        for d in (1, 2, 3):
            peer = {"zh": shifted("zh", d)}
            send(share.at[0], share.at[d], per[k][12].at[1], per[k][13].at[1], peer)

    def spread_residual(k):
        share, measured = per[k][6], per[k][7]
        await_bytes(share.at[pl.ds(1, 3)], per[k][13].at[1])
        value = (share[0] + share[1]) + (share[2] + share[3])
        square = value * value
        excess = square + swapped(square, F32(1)) - measured[...]
        share[4] = excess * value * F32(1 / 256)
        mine = gathered(k).at[own_rows, :]
        for dx, dc in XC:
            peer = {"x": shifted("x", dx), "c": shifted("c", dc)}
            send(share.at[4], mine, per[k][12].at[2], per[k][13].at[2], peer)
        pltpu.make_async_copy(share.at[4], mine, out_sems.at[k]).start()

    def gathered(k):
        return per[k][3].at[: 8 * rows, :] if k < n - 1 else res_out

    def await_residual(k):
        await_bytes(per[k][5], per[k][13].at[2])
        await_bytes(per[k][6].at[4], out_sems.at[k])

    def gradient(k, add):
        await_residual(k)
        high, low = stacked_residual(per[k][3][: 8 * rows, :])
        sh, sl = per[k][1], per[k][2]
        for g in range(4):
            value = dot3(high, low, sh[g], sl[g], 1).reshape(2, 8 * rows, 384)
            if add:
                grad[:, :, g * 384 : (g + 1) * 384] += value
            else:
                grad[:, :, g * 384 : (g + 1) * 384] = value

    def drain(k):
        await_bytes(per[k][0].at[pl.ds(0, 15)], per[k][8])
        await_bytes(per[k][5], per[k][12].at[0])
        await_bytes(per[k][6].at[pl.ds(0, 3)], per[k][12].at[1])
        await_bytes(per[k][5], per[k][12].at[2])

    for k in range(n):
        issue(k)

    u_copy.wait()
    for g in range(4):
        for p in range(2):
            high, low = halves(uf[p, :, g * 384 : (g + 1) * 384])
            uh[g, p * 192 : (p + 1) * 192, :] = high
            ul[g, p * 192 : (p + 1) * 192, :] = low

    gather(0)
    forward_all(1)
    fields(0)
    spread_fields(0)
    relay_all(1)
    forward_all(2)
    fields(1)
    spread_fields(1)
    relay_all(2)
    sum_over_x(0)
    fields(2)
    spread_fields(2)
    keep_h = pltpu.make_async_copy(per[n - 1][1], last_h, out_sems.at[3])
    keep_l = pltpu.make_async_copy(per[n - 1][2], last_l, out_sems.at[4])
    keep_h.start()
    keep_l.start()
    sum_over_x(1)
    spread_residual(0)
    sum_over_x(2)
    spread_residual(1)
    gradient(0, False)
    gradient(1, True)
    keep_grad = pltpu.make_async_copy(grad, grad_out, out_sems.at[5])
    keep_grad.start()
    spread_residual(2)
    keep_h.wait()
    keep_l.wait()
    keep_grad.wait()
    drain(0)
    drain(1)
    drain(2)
    await_residual(2)


def finish_kernel(grad, res, last_h, last_l, out, done, sems):
    high, low = stacked_residual(res[...])
    copies = []
    for g in range(4):
        value = dot3(high, low, last_h[g], last_l[g], 1)
        columns = pl.ds(g * 384, 384)
        done[:, :, columns] = grad[:, :, columns] + value.reshape(2, value.shape[0] // 2, 384)
        copy = pltpu.make_async_copy(done.at[:, :, columns], out.at[:, :, columns], sems.at[g])
        copy.start()
        copies.append(copy)
    for copy in copies:
        copy.wait()


def body(transfer_matrix, probes, intensity):
    _, m, cols = transfer_matrix.shape
    rows = m // 8
    width = CHUNKS[-1][1]
    vmem = pl.BlockSpec(memory_space=pltpu.VMEM)
    hbm = pl.BlockSpec(memory_space=pltpu.HBM)
    scratch = [
        pltpu.VMEM((2, m, cols), F32),
        pltpu.VMEM((4, 2 * m, cols // 4), BF16),
        pltpu.VMEM((4, 2 * m, cols // 4), BF16),
        pltpu.VMEM(probes.shape, F32),
        pltpu.VMEM((rows, intensity.shape[1]), F32),
        pltpu.VMEM((2, m, cols), F32),
        pltpu.SemaphoreType.DMA((3,)),
        pltpu.SemaphoreType.DMA((6,)),
        pltpu.SemaphoreType.REGULAR((3,)),
    ]
    for _, w in CHUNKS:
        scratch += [
            pltpu.VMEM((16, 2, 48, 2 * w), F32),
            pltpu.VMEM((4, cols // 4, 2 * w), BF16),
            pltpu.VMEM((4, cols // 4, 2 * w), BF16),
            pltpu.VMEM((2 * m, 2 * w), F32),
            pltpu.VMEM((8, rows, 2 * w), F32),
            pltpu.VMEM((7, rows, 2 * w), F32),
            pltpu.VMEM((5, rows, 2 * w), F32),
            pltpu.VMEM((rows, 2 * w), F32),
            pltpu.SemaphoreType.DMA,
            pltpu.SemaphoreType.DMA((3,)),
            pltpu.SemaphoreType.DMA((4,)),
            pltpu.SemaphoreType.DMA((4,)),
            pltpu.SemaphoreType.DMA((3,)),
            pltpu.SemaphoreType.DMA((3,)),
        ]
    outs = pl.pallas_call(
        gather_kernel,
        out_shape=(
            jax.ShapeDtypeStruct((2, m, cols), F32),
            jax.ShapeDtypeStruct((m, 2 * width), F32),
            jax.ShapeDtypeStruct((4, cols // 4, 2 * width), BF16),
            jax.ShapeDtypeStruct((4, cols // 4, 2 * width), BF16),
        ),
        in_specs=[hbm] * 3,
        out_specs=(pl.BlockSpec(memory_space=pl.ANY),) * 4,
        scratch_shapes=scratch,
        compiler_params=pltpu.CompilerParams(
            collective_id=0, has_side_effects=True, vmem_limit_bytes=32 * 1024 * 1024
        ),
        name="gather",
    )(*(pltpu.with_memory_space_constraint(a, pltpu.HBM) for a in (transfer_matrix, probes, intensity)))
    return pl.pallas_call(
        finish_kernel,
        out_shape=jax.ShapeDtypeStruct((2, m, cols), F32),
        in_specs=[vmem] * 4,
        out_specs=hbm,
        scratch_shapes=[pltpu.VMEM((2, m, cols), F32), pltpu.SemaphoreType.DMA((4,))],
        compiler_params=pltpu.CompilerParams(vmem_limit_bytes=32 * 1024 * 1024),
        name="finish",
    )(*outs)


def solution(mesh):
    split = Mesh(mesh.devices.reshape([SIZES[a] for a in AXES]), AXES)
    row, mode = ("zl", "y"), ("zh", "x", "c")
    placed = (P(None, row, mode), P(None, mode + row, None), P(row, None))
    return jax.shard_map(
        body, mesh=split, in_specs=placed, out_specs=P(None, row, mode), check_vma=False
    )
```

```python
import jax
import jax.numpy as jnp
from jax import lax
from jax.experimental import pallas as pl
from jax.experimental.pallas import tpu as pltpu
from jax.sharding import Mesh
from jax.sharding import PartitionSpec as P

AXES = ("zl", "y", "zh", "x", "c")
SIZES = {"zl": 4, "y": 4, "zh": 4, "x": 4, "c": 2}
CHUNKS = ((0, 128), (128, 64), (192, 64))
BY_MESH = pl.DeviceIdType.MESH
XC = tuple((dx, dc) for dx in range(4) for dc in range(2) if (dx, dc) != (0, 0))
F32, BF16 = jnp.float32, jnp.bfloat16


def shifted(axis, by):
    return lax.rem(lax.axis_index(axis) + by, SIZES[axis])


def along_z(by):
    z = lax.rem(lax.axis_index("zh") * 4 + lax.axis_index("zl") + (by + 16), 16)
    return {"zh": lax.div(z, 4), "zl": lax.rem(z, 4)}


def partner(index, j):
    if j == 0:
        return index
    if j == 1:
        return index + 1 - 2 * lax.rem(index, 2)
    if j == 2:
        return lax.rem(index + 2, 4)
    return 3 - index


def halves(value):
    high = value.astype(BF16)
    return high, (value - high.astype(F32)).astype(BF16)


def dot3(a_high, a_low, b_high, b_low, contract_b):
    dims = (((1,), (contract_b,)), ((), ()))

    def dot(a, b):
        return lax.dot_general(a, b, dims, preferred_element_type=F32)

    return dot(a_high, b_high) + (dot(a_high, b_low) + dot(a_low, b_high))


def swapped(value, signs):
    width = value.shape[1] // 2
    if width % 128 == 0:
        turned = jnp.concatenate([value[:, width:], value[:, :width]], axis=1)
    else:
        turned = pltpu.roll(value, width, 1)
    return turned * signs


def sign_row(width, first, second):
    lane = lax.broadcasted_iota(jnp.int32, (1, 2 * width), 1)
    return jnp.where(lane < width, F32(first), F32(second))


def stacked_residual(value, chunks):
    size = value.shape[1] // chunks
    signs = sign_row(size // 2, 1, -1)
    turned = [swapped(value[:, i * size : (i + 1) * size], signs) for i in range(chunks)]
    return halves(jnp.concatenate([value, jnp.concatenate(turned, axis=1)], axis=0))


def gather_kernel(u_hbm, s_hbm, i_hbm, *rest):
    n = len(CHUNKS)
    grad, res_out, last_h, last_l = rest[:4]
    uf, uh, ul, s_ref, i_ref, sh0, sl0, in_sems, out_sems, near, b_sems = rest[4:15]
    per = [rest[15 + 12 * k : 15 + 12 * (k + 1)] for k in range(n)]
    zl, y, x, c = (lax.axis_index(a) for a in ("zl", "y", "x", "c"))
    own = x * 2 + c
    up, down = shifted("y", 1), shifted("y", 3)
    rows = i_ref.shape[0]
    own_rows = pl.ds(pl.multiple_of(own * rows, 8), rows)

    s_copy = pltpu.make_async_copy(s_hbm, s_ref, in_sems.at[0])
    i_copy = pltpu.make_async_copy(i_hbm.at[own_rows, :], i_ref, in_sems.at[1])
    u_copy = pltpu.make_async_copy(u_hbm, uf, in_sems.at[2])
    s_copy.start()
    i_copy.start()
    u_copy.start()

    barrier = pltpu.get_barrier_semaphore()
    peers = [{"zl": partner(zl, j)} for j in (1, 2, 3)]
    peers += [{"y": up}, {"y": down}]
    peers += [{"x": shifted("x", dx), "c": shifted("c", dc)} for dx, dc in XC]
    peers += [along_z(1), along_z(-1)]
    for peer in peers:
        pl.semaphore_signal(barrier, inc=1, device_id=peer, device_id_type=BY_MESH)

    s_copy.wait()
    i_copy.wait()
    for k, (first, width) in enumerate(CHUNKS):
        strip = per[k][0]
        packed = jnp.concatenate(
            [s_ref[0, :, first : first + width], s_ref[1, :, first : first + width]], axis=1
        )
        strip[zl * 4 + y] = packed.reshape(2, 48, 2 * width)
        mine = i_ref[:, first : first + width]
        per[k][5][...] = jnp.concatenate([mine, mine], axis=1)

    pl.semaphore_wait(barrier, len(peers))

    def announce(i):
        for by in (1 << i, -(1 << i)):
            pl.semaphore_signal(near.at[i], inc=1, device_id=along_z(by), device_id_type=BY_MESH)

    def heard(i):
        pl.semaphore_wait(near.at[i], 2)

    announce(0)

    def send(src, dst, send_sem, recv_sem, peer):
        pltpu.make_async_remote_copy(
            src_ref=src, dst_ref=dst, send_sem=send_sem, recv_sem=recv_sem,
            device_id=peer, device_id_type=BY_MESH,
        ).start()

    def await_bytes(of, sem):
        pltpu.make_async_copy(of, of, sem).wait()

    def place(j, at):
        return partner(zl, j) * 4 + at

    def part(k, at):
        strip = per[k][0]
        return strip.at[at] if k < n - 1 else strip.at[at, 0]

    def part_half(k, at, h):
        strip = per[k][0]
        return strip.at[at, h] if k < n - 1 else strip.at[at, 0, pl.ds(24 * h, 24)]

    def parts_like(k, count):
        strip = per[k][0]
        return strip.at[pl.ds(0, count)] if k < n - 1 else strip.at[pl.ds(0, count), 0]

    def both_ways(k, j):
        sem, arrived = per[k][6], per[k][8].at[j]
        block = part(k, place(j, y))
        send(block, block, sem, arrived, {"y": up})
        send(block, block, sem, arrived, {"y": down})
        if direct(k, j):
            send(block, block, sem, per[k][9].at[j], {"y": shifted("y", 2)})

    def direct(k, j):
        return k == n - 1 and j == 3

    def issue(k):
        sem, arrived = per[k][6], per[k][7]
        block = part(k, place(0, y))
        for j in (1, 2, 3):
            send(block, block, sem, arrived.at[j - 1], {"zl": partner(zl, j)})
        both_ways(k, 0)
        if k == n - 1:
            turn(up)
            turn(down)

    def turn(to):
        block = per[n - 1][0].at[place(0, y), 1]
        send(block, block, per[n - 1][6], b_sems.at[0], {"y": to})

    def cross():
        strip, sem = per[n - 1][0], per[n - 1][6]
        await_bytes(strip.at[pl.ds(0, 3), 1], b_sems.at[0])
        column = strip.at[pl.ds(zl * 4, 4), 1]
        for j in (1, 2, 3):
            send(column, column, sem, b_sems.at[j], {"zl": partner(zl, j)})

    def relay(k, j):
        sem, arrived = per[k][6], per[k][9].at[j]
        await_bytes(parts_like(k, 2), per[k][8].at[j])
        if not direct(k, j):
            from_down = part_half(k, place(j, down), 0)
            from_up = part_half(k, place(j, up), 1)
            send(from_down, from_down, sem, arrived, {"y": up})
            send(from_up, from_up, sem, arrived, {"y": down})

    def forward(k, j):
        await_bytes(part(k, 0), per[k][7].at[j - 1])
        both_ways(k, j)

    def relay_rest(k):
        for j in (1, 2, 3):
            relay(k, j)

    def forward_all(k):
        for j in (1, 2, 3):
            forward(k, j)

    def gather_first():
        for j in (0, 1, 2, 3):
            if j < 3:
                forward(0, j + 1)
                heard(j)
                if j < 2:
                    announce(j + 1)
                else:
                    cross()
            relay(0, j)
            if j == 0:
                turn(shifted("y", 2))
            if j < 2:
                relay(j + 1, 0)

    def fields(k):
        strip, total = per[k][:2]
        width = CHUNKS[k][1]
        for j in (0, 1, 2, 3):
            await_bytes(part(k, 0), per[k][9].at[j])
            if k == n - 1 and j > 0:
                await_bytes(strip.at[pl.ds(0, 4), 1], b_sems.at[j])
            g = partner(zl, j)
            value = strip[pl.ds(pl.multiple_of(g * 4, 4), 4)]
            high, low = halves(value.reshape(384, 2 * width))
            keep_high, keep_low, lanes = kept(k)
            keep_high[g, :, lanes] = high
            keep_low[g, :, lanes] = low
            value = dot3(uh[g], ul[g], high, low, 0)
            if j == 0:
                total[...] = value
            else:
                total[...] += value

    def spread_fields(k):
        total, parts, got = per[k][1:4]
        width = CHUNKS[k][1]
        half = total.shape[0] // 2
        value = total[:half, :] + swapped(total[half:, :], sign_row(width, -1, 1))
        parts[...] = value.reshape(parts.shape)
        for i, (dx, dc) in enumerate(XC):
            tx, tc = shifted("x", dx), shifted("c", dc)
            part = parts.at[tx * 2 + tc]
            send(part, got.at[i], per[k][10].at[0], per[k][11].at[0], {"x": tx, "c": tc})

    def sum_over_x(k):
        parts, got, share = per[k][2], per[k][3], per[k][4]
        await_bytes(got, per[k][11].at[0])
        value = parts[own]
        for i in range(7):
            value = value + got[i]
        share[0] = value
        for d in (1, 2, 3):
            peer = {"zh": shifted("zh", d)}
            send(share.at[0], share.at[d], per[k][10].at[1], per[k][11].at[1], peer)

    def spread_residual(k):
        share, measured = per[k][4], per[k][5]
        await_bytes(share.at[pl.ds(1, 3)], per[k][11].at[1])
        value = (share[0] + share[1]) + (share[2] + share[3])
        square = value * value
        excess = square + swapped(square, F32(1)) - measured[...]
        share[4] = excess * value * F32(1 / 256)
        mine = gathered(k).at[own_rows, :]
        for dx, dc in XC:
            peer = {"x": shifted("x", dx), "c": shifted("c", dc)}
            send(share.at[4], mine, per[k][10].at[2], per[k][11].at[2], peer)
        pltpu.make_async_copy(share.at[4], mine, out_sems.at[k]).start()

    def kept(k):
        if k == 0:
            return sh0, sl0, slice(None)
        return last_h, last_l, pl.ds(128 * (k - 1), 128)

    def gathered(k):
        return per[0][1].at[: 8 * rows, :] if k == 0 else res_out.at[:, pl.ds(128 * (k - 1), 128)]

    def await_residual(k):
        await_bytes(per[k][3], per[k][11].at[2])
        await_bytes(per[k][4].at[4], out_sems.at[k])

    def gradient_first():
        await_residual(0)
        high, low = stacked_residual(per[0][1][: 8 * rows, :], 1)
        for g in range(4):
            value = dot3(high, low, sh0[g], sl0[g], 1).reshape(2, 8 * rows, 384)
            grad[:, :, g * 384 : (g + 1) * 384] = value

    def drain(k):
        await_bytes(per[k][0].at[pl.ds(0, 15)], per[k][6])
        await_bytes(per[k][3], per[k][10].at[0])
        await_bytes(per[k][4].at[pl.ds(0, 3)], per[k][10].at[1])
        await_bytes(per[k][3], per[k][10].at[2])

    for k in range(n):
        issue(k)

    u_copy.wait()
    for g in range(4):
        for p in range(2):
            high, low = halves(uf[p, :, g * 384 : (g + 1) * 384])
            uh[g, p * 192 : (p + 1) * 192, :] = high
            ul[g, p * 192 : (p + 1) * 192, :] = low

    gather_first()
    forward_all(1)
    forward_all(2)
    fields(0)
    spread_fields(0)
    relay_rest(1)
    relay_rest(2)
    fields(1)
    spread_fields(1)
    sum_over_x(0)
    fields(2)
    spread_fields(2)
    sum_over_x(1)
    sum_over_x(2)
    spread_residual(0)
    spread_residual(1)
    gradient_first()
    spread_residual(2)
    for k in range(n):
        drain(k)
    await_residual(1)
    await_residual(2)


def finish_kernel(grad, res, last_h, last_l, out, done, sems):
    high, low = stacked_residual(res[...], 2)
    copies = []
    for g in range(4):
        value = dot3(high, low, last_h[g], last_l[g], 1)
        columns = pl.ds(g * 384, 384)
        done[:, :, columns] = grad[:, :, columns] + value.reshape(2, value.shape[0] // 2, 384)
        copy = pltpu.make_async_copy(done.at[:, :, columns], out.at[:, :, columns], sems.at[g])
        copy.start()
        copies.append(copy)
    for copy in copies:
        copy.wait()


def body(transfer_matrix, probes, intensity):
    _, m, cols = transfer_matrix.shape
    rows = m // 8
    width = CHUNKS[1][1] + CHUNKS[2][1]
    vmem = pl.BlockSpec(memory_space=pltpu.VMEM)
    hbm = pl.BlockSpec(memory_space=pltpu.HBM)
    scratch = [
        pltpu.VMEM((2, m, cols), F32),
        pltpu.VMEM((4, 2 * m, cols // 4), BF16),
        pltpu.VMEM((4, 2 * m, cols // 4), BF16),
        pltpu.VMEM(probes.shape, F32),
        pltpu.VMEM((rows, intensity.shape[1]), F32),
        pltpu.VMEM((4, cols // 4, 2 * CHUNKS[0][1]), BF16),
        pltpu.VMEM((4, cols // 4, 2 * CHUNKS[0][1]), BF16),
        pltpu.SemaphoreType.DMA((3,)),
        pltpu.SemaphoreType.DMA((3,)),
        pltpu.SemaphoreType.REGULAR((3,)),
        pltpu.SemaphoreType.DMA((4,)),
    ]
    for _, w in CHUNKS:
        scratch += [
            pltpu.VMEM((16, 2, 48, 2 * w), F32),
            pltpu.VMEM((2 * m, 2 * w), F32),
            pltpu.VMEM((8, rows, 2 * w), F32),
            pltpu.VMEM((7, rows, 2 * w), F32),
            pltpu.VMEM((5, rows, 2 * w), F32),
            pltpu.VMEM((rows, 2 * w), F32),
            pltpu.SemaphoreType.DMA,
            pltpu.SemaphoreType.DMA((3,)),
            pltpu.SemaphoreType.DMA((4,)),
            pltpu.SemaphoreType.DMA((4,)),
            pltpu.SemaphoreType.DMA((3,)),
            pltpu.SemaphoreType.DMA((3,)),
        ]
    outs = pl.pallas_call(
        gather_kernel,
        out_shape=(
            jax.ShapeDtypeStruct((2, m, cols), F32),
            jax.ShapeDtypeStruct((m, 2 * width), F32),
            jax.ShapeDtypeStruct((4, cols // 4, 2 * width), BF16),
            jax.ShapeDtypeStruct((4, cols // 4, 2 * width), BF16),
        ),
        in_specs=[hbm] * 3,
        out_specs=(vmem,) * 4,
        scratch_shapes=scratch,
        compiler_params=pltpu.CompilerParams(
            collective_id=0, has_side_effects=True, vmem_limit_bytes=32 * 1024 * 1024
        ),
        name="gather",
    )(*(pltpu.with_memory_space_constraint(a, pltpu.HBM) for a in (transfer_matrix, probes, intensity)))
    return pl.pallas_call(
        finish_kernel,
        out_shape=jax.ShapeDtypeStruct((2, m, cols), F32),
        in_specs=[vmem] * 4,
        out_specs=hbm,
        scratch_shapes=[pltpu.VMEM((2, m, cols), F32), pltpu.SemaphoreType.DMA((4,))],
        compiler_params=pltpu.CompilerParams(vmem_limit_bytes=32 * 1024 * 1024),
        name="finish",
    )(*outs)


def solution(mesh):
    split = Mesh(mesh.devices.reshape([SIZES[a] for a in AXES]), AXES)
    row, mode = ("zl", "y"), ("zh", "x", "c")
    placed = (P(None, row, mode), P(None, mode + row, None), P(row, None))
    return jax.shard_map(
        body, mesh=split, in_specs=placed, out_specs=P(None, row, mode), check_vma=False
    )
```

```python
import jax
import jax.numpy as jnp
from jax import lax
from jax.experimental import pallas as pl
from jax.experimental.pallas import tpu as pltpu
from jax.sharding import Mesh
from jax.sharding import PartitionSpec as P

AXES = ("zl", "y", "zh", "x", "c")
SIZES = {"zl": 4, "y": 4, "zh": 4, "x": 4, "c": 2}
CHUNKS = ((0, 128), (128, 64), (192, 64))
FIRST_ROWS = 48
BY_MESH = pl.DeviceIdType.MESH
XC = tuple((dx, dc) for dx in range(4) for dc in range(2) if (dx, dc) != (0, 0))
F32, BF16 = jnp.float32, jnp.bfloat16


def shifted(axis, by):
    return lax.rem(lax.axis_index(axis) + by, SIZES[axis])


def along_z(by):
    z = lax.rem(lax.axis_index("zh") * 4 + lax.axis_index("zl") + (by + 16), 16)
    return {"zh": lax.div(z, 4), "zl": lax.rem(z, 4)}


def partner(index, j):
    if j == 0:
        return index
    if j == 1:
        return index + 1 - 2 * lax.rem(index, 2)
    if j == 2:
        return lax.rem(index + 2, 4)
    return 3 - index


def halves(value):
    high = value.astype(BF16)
    return high, (value - high.astype(F32)).astype(BF16)


def dot(a, b, contract_b):
    dims = (((1,), (contract_b,)), ((), ()))
    return lax.dot_general(a, b, dims, preferred_element_type=F32)


def fields_dot(a_high, a_low, high, low):
    width = high.shape[1]
    if width < 256:
        both = dot(a_high, jnp.concatenate([high, low], axis=1), 0)
        main, cross = both[:, :width], both[:, width:]
    else:
        main, cross = dot(a_high, high, 0), dot(a_high, low, 0)
    return main + (cross + dot(a_low, high, 0))


def gradient_dot(a_high, a_low, high, low):
    if high.shape[1] < 256:
        main = dot(
            jnp.concatenate([a_high, a_low], axis=1), jnp.concatenate([high, high], axis=1), 1
        )
    else:
        main = dot(a_high, high, 1) + dot(a_low, high, 1)
    return main + dot(a_high, low, 1)


def swapped(value, signs):
    width = value.shape[1] // 2
    if width % 128 == 0:
        turned = jnp.concatenate([value[:, width:], value[:, :width]], axis=1)
    else:
        turned = pltpu.roll(value, width, 1)
    return turned * signs


def sign_row(width, first, second):
    lane = lax.broadcasted_iota(jnp.int32, (1, 2 * width), 1)
    return jnp.where(lane < width, F32(first), F32(second))


def stacked_residual(value):
    turned = swapped(value, sign_row(value.shape[1] // 2, 1, -1))
    return halves(jnp.concatenate([value, turned], axis=0))


def gather_kernel(u_hbm, s_hbm, i_hbm, *rest):
    n = len(CHUNKS)
    grad, res_out, last_h, last_l = rest[:4]
    uf, uh, ul, s_ref, i_ref, sh0, sl0, sh1, sl1, in_sems, out_sems, near, b_sems = rest[4:17]
    per = [rest[17 + 12 * k : 17 + 12 * (k + 1)] for k in range(n)]
    zl, y, x, c = (lax.axis_index(a) for a in ("zl", "y", "x", "c"))
    own = x * 2 + c
    up, down = shifted("y", 1), shifted("y", 3)
    rows = i_ref.shape[0]
    own_rows = pl.ds(pl.multiple_of(own * rows, 8), rows)

    s_copy = pltpu.make_async_copy(s_hbm, s_ref, in_sems.at[0])
    i_copy = pltpu.make_async_copy(i_hbm.at[own_rows, :], i_ref, in_sems.at[1])
    u_copy = pltpu.make_async_copy(u_hbm, uf, in_sems.at[2])
    s_copy.start()
    i_copy.start()
    u_copy.start()

    barrier = pltpu.get_barrier_semaphore()
    beside = [{"x": shifted("x", 1)}, {"x": shifted("x", 3)}]
    twin = {"c": 1 - c}
    peers = [{"zl": partner(zl, j)} for j in (1, 2, 3)]
    peers += [{"y": up}, {"y": down}, along_z(1), along_z(-1), twin] + beside
    for peer in peers:
        pl.semaphore_signal(barrier, inc=1, device_id=peer, device_id_type=BY_MESH)

    s_copy.wait()
    i_copy.wait()
    for k, (first, width) in enumerate(CHUNKS):
        strip = per[k][0]
        packed = jnp.concatenate(
            [s_ref[0, :, first : first + width], s_ref[1, :, first : first + width]], axis=1
        )
        strip[zl * 4 + y] = packed
        mine = i_ref[:, first : first + width]
        per[k][5][...] = jnp.concatenate([mine, mine], axis=1)

    pl.semaphore_wait(barrier, len(peers))

    def announce(i):
        for by in (1 << i, -(1 << i)):
            pl.semaphore_signal(near.at[i], inc=1, device_id=along_z(by), device_id_type=BY_MESH)

    def heard(i):
        pl.semaphore_wait(near.at[i], 2)

    def announce_x(i):
        for peer in beside + [twin][i:]:
            pl.semaphore_signal(near.at[3 + i], inc=1, device_id=peer, device_id_type=BY_MESH)

    def heard_x(i):
        pl.semaphore_wait(near.at[3 + i], 3 - i)

    announce(0)
    announce_x(0)

    def send(src, dst, send_sem, recv_sem, peer):
        pltpu.make_async_remote_copy(
            src_ref=src, dst_ref=dst, send_sem=send_sem, recv_sem=recv_sem,
            device_id=peer, device_id_type=BY_MESH,
        ).start()

    def await_bytes(of, sem):
        pltpu.make_async_copy(of, of, sem).wait()

    def place(j, at):
        return partner(zl, j) * 4 + at

    def leading(k):
        return per[k][0].shape[1] if k < n - 1 else FIRST_ROWS

    trailing = pl.ds(FIRST_ROWS, per[n - 1][0].shape[1] - FIRST_ROWS)

    def part(k, at):
        return per[k][0].at[at, pl.ds(0, leading(k))]

    def part_half(k, at, h):
        size = leading(k) // 2
        return per[k][0].at[at, pl.ds(size * h, size)]

    def parts_like(k, count):
        return per[k][0].at[pl.ds(0, count), pl.ds(0, leading(k))]

    def both_ways(k, j):
        sem, arrived = per[k][6], per[k][8].at[j]
        block = part(k, place(j, y))
        send(block, block, sem, arrived, {"y": up})
        send(block, block, sem, arrived, {"y": down})
        if direct(k, j):
            send(block, block, sem, per[k][9].at[j], {"y": shifted("y", 2)})

    def direct(k, j):
        return k == n - 1 and j > 0

    def issue(k):
        sem, arrived = per[k][6], per[k][7]
        block = part(k, place(0, y))
        for j in (1, 2, 3):
            send(block, block, sem, arrived.at[j - 1], {"zl": partner(zl, j)})
        both_ways(k, 0)
        if k == n - 1:
            turn(up)
            turn(down)

    def turn(to):
        block = per[n - 1][0].at[place(0, y), trailing]
        send(block, block, per[n - 1][6], b_sems.at[0], {"y": to})

    def cross():
        strip, sem = per[n - 1][0], per[n - 1][6]
        await_bytes(strip.at[pl.ds(0, 3), trailing], b_sems.at[0])
        column = strip.at[pl.ds(zl * 4, 4), trailing]
        for j in (1, 2, 3):
            send(column, column, sem, b_sems.at[j], {"zl": partner(zl, j)})

    def relay(k, j):
        sem, arrived = per[k][6], per[k][9].at[j]
        await_bytes(parts_like(k, 2), per[k][8].at[j])
        if not direct(k, j):
            from_down = part_half(k, place(j, down), 0)
            from_up = part_half(k, place(j, up), 1)
            send(from_down, from_down, sem, arrived, {"y": up})
            send(from_up, from_up, sem, arrived, {"y": down})

    def forward(k, j):
        await_bytes(part(k, 0), per[k][7].at[j - 1])
        both_ways(k, j)

    def relay_rest(k):
        for j in (1, 2, 3):
            relay(k, j)

    def forward_all(k):
        for j in (1, 2, 3):
            forward(k, j)

    def gather_first():
        for j in (0, 1, 2, 3):
            if j < 3:
                forward(0, j + 1)
            if j < 3:
                heard(j)
            if j < 2:
                announce(j + 1)
            if j == 2:
                cross()
            relay(0, j)
            if j == 0:
                turn(shifted("y", 2))
            if j < 2:
                relay(j + 1, 0)
                heard_x(j)
            if j == 0:
                announce_x(1)

    def fields(k, t):
        strip, total = per[k][:2]
        width = CHUNKS[k][1]
        keep_high, keep_low = kept(k)
        for j in (2 * t, 2 * t + 1):
            await_bytes(part(k, 0), per[k][9].at[j])
            if k == n - 1 and j > 0:
                await_bytes(strip.at[pl.ds(0, 4), trailing], b_sems.at[j])
        q = lax.div(zl, 2) if t == 0 else 1 - lax.div(zl, 2)
        high, low = halves(strip[pl.ds(q * 8, 8)].reshape(768, 2 * width))
        keep_high[q] = high
        keep_low[q] = low
        value = fields_dot(uh[q], ul[q], high, low)
        if t == 0:
            total[...] = value
        else:
            total[...] += value

    def spread_fields(k):
        total, parts, got = per[k][1:4]
        width = CHUNKS[k][1]
        half = total.shape[0] // 2
        value = total[:half, :] + swapped(total[half:, :], sign_row(width, -1, 1))
        parts[...] = value.reshape(parts.shape)
        for i, (dx, dc) in enumerate(XC):
            tx, tc = shifted("x", dx), shifted("c", dc)
            part = parts.at[tx * 2 + tc]
            send(part, got.at[i], per[k][10].at[0], per[k][11].at[0], {"x": tx, "c": tc})

    def sum_over_x(k):
        parts, got, share = per[k][2], per[k][3], per[k][4]
        await_bytes(got, per[k][11].at[0])
        value = parts[own]
        for i in range(7):
            value = value + got[i]
        share[0] = value
        for d in (1, 2, 3):
            peer = {"zh": shifted("zh", d)}
            send(share.at[0], share.at[d], per[k][10].at[1], per[k][11].at[1], peer)

    def spread_residual(k):
        share, measured = per[k][4], per[k][5]
        await_bytes(share.at[pl.ds(1, 3)], per[k][11].at[1])
        value = (share[0] + share[1]) + (share[2] + share[3])
        square = value * value
        excess = square + swapped(square, F32(1)) - measured[...]
        share[4] = excess * value * F32(1 / 256)
        mine = gathered(k).at[own_rows, :]
        for dx, dc in XC:
            peer = {"x": shifted("x", dx), "c": shifted("c", dc)}
            send(share.at[4], mine, per[k][10].at[2], per[k][11].at[2], peer)
        pltpu.make_async_copy(share.at[4], mine, out_sems.at[k]).start()

    def kept(k):
        return ((sh0, sl0), (sh1, sl1), (last_h, last_l))[k]

    def gathered(k):
        return per[k][1].at[: 8 * rows, :] if k < n - 1 else res_out

    def await_residual(k):
        await_bytes(per[k][3], per[k][11].at[2])
        await_bytes(per[k][4].at[4], out_sems.at[k])

    def gradient(k):
        await_residual(k)
        high, low = stacked_residual(per[k][1][: 8 * rows, :])
        keep_high, keep_low = kept(k)
        for q in range(2):
            value = gradient_dot(high, low, keep_high[q], keep_low[q]).reshape(2, 8 * rows, 768)
            if k == 0:
                grad[:, :, q * 768 : (q + 1) * 768] = value
            else:
                grad[:, :, q * 768 : (q + 1) * 768] += value

    def drain(k):
        await_bytes(per[k][0].at[pl.ds(0, 15)], per[k][6])
        await_bytes(per[k][3], per[k][10].at[0])
        await_bytes(per[k][4].at[pl.ds(0, 3)], per[k][10].at[1])
        await_bytes(per[k][3], per[k][10].at[2])

    for k in range(n):
        issue(k)

    u_copy.wait()
    for q in range(2):
        for p in range(2):
            high, low = halves(uf[p, :, q * 768 : (q + 1) * 768])
            uh[q, p * 192 : (p + 1) * 192, :] = high
            ul[q, p * 192 : (p + 1) * 192, :] = low

    gather_first()
    forward_all(1)
    fields(0, 0)
    fields(0, 1)
    spread_fields(0)
    relay_rest(1)
    forward_all(2)
    fields(1, 0)
    fields(1, 1)
    spread_fields(1)
    relay_rest(2)
    sum_over_x(0)
    fields(2, 0)
    fields(2, 1)
    spread_fields(2)
    sum_over_x(1)
    sum_over_x(2)
    spread_residual(0)
    spread_residual(1)
    spread_residual(2)
    gradient(0)
    gradient(1)
    for k in range(n):
        drain(k)
    await_residual(2)


def finish_kernel(grad, res, last_h, last_l, out, done, sems):
    high, low = stacked_residual(res[...])
    copies = []
    for g in range(6):
        of = (g // 3, pl.ds(g % 3 * 256, 256))
        value = gradient_dot(high, low, last_h[of], last_l[of])
        columns = pl.ds(g * 256, 256)
        done[:, :, columns] = grad[:, :, columns] + value.reshape(2, value.shape[0] // 2, 256)
        copy = pltpu.make_async_copy(done.at[:, :, columns], out.at[:, :, columns], sems.at[g])
        copy.start()
        copies.append(copy)
    for copy in copies:
        copy.wait()


def body(transfer_matrix, probes, intensity):
    _, m, cols = transfer_matrix.shape
    rows = m // 8
    width = CHUNKS[-1][1]
    vmem = pl.BlockSpec(memory_space=pltpu.VMEM)
    hbm = pl.BlockSpec(memory_space=pltpu.HBM)
    scratch = [
        pltpu.VMEM((2, m, cols), F32),
        pltpu.VMEM((2, 2 * m, cols // 2), BF16),
        pltpu.VMEM((2, 2 * m, cols // 2), BF16),
        pltpu.VMEM(probes.shape, F32),
        pltpu.VMEM((rows, intensity.shape[1]), F32),
        pltpu.VMEM((2, cols // 2, 2 * CHUNKS[0][1]), BF16),
        pltpu.VMEM((2, cols // 2, 2 * CHUNKS[0][1]), BF16),
        pltpu.VMEM((2, cols // 2, 2 * CHUNKS[1][1]), BF16),
        pltpu.VMEM((2, cols // 2, 2 * CHUNKS[1][1]), BF16),
        pltpu.SemaphoreType.DMA((3,)),
        pltpu.SemaphoreType.DMA((3,)),
        pltpu.SemaphoreType.REGULAR((5,)),
        pltpu.SemaphoreType.DMA((4,)),
    ]
    for _, w in CHUNKS:
        scratch += [
            pltpu.VMEM((16, cols // 16, 2 * w), F32),
            pltpu.VMEM((2 * m, 2 * w), F32),
            pltpu.VMEM((8, rows, 2 * w), F32),
            pltpu.VMEM((7, rows, 2 * w), F32),
            pltpu.VMEM((5, rows, 2 * w), F32),
            pltpu.VMEM((rows, 2 * w), F32),
            pltpu.SemaphoreType.DMA,
            pltpu.SemaphoreType.DMA((3,)),
            pltpu.SemaphoreType.DMA((4,)),
            pltpu.SemaphoreType.DMA((4,)),
            pltpu.SemaphoreType.DMA((3,)),
            pltpu.SemaphoreType.DMA((3,)),
        ]
    outs = pl.pallas_call(
        gather_kernel,
        out_shape=(
            jax.ShapeDtypeStruct((2, m, cols), F32),
            jax.ShapeDtypeStruct((m, 2 * width), F32),
            jax.ShapeDtypeStruct((2, cols // 2, 2 * width), BF16),
            jax.ShapeDtypeStruct((2, cols // 2, 2 * width), BF16),
        ),
        in_specs=[hbm] * 3,
        out_specs=(vmem,) * 4,
        scratch_shapes=scratch,
        compiler_params=pltpu.CompilerParams(
            collective_id=0, has_side_effects=True, vmem_limit_bytes=32 * 1024 * 1024
        ),
        name="gather",
    )(*(pltpu.with_memory_space_constraint(a, pltpu.HBM) for a in (transfer_matrix, probes, intensity)))
    return pl.pallas_call(
        finish_kernel,
        out_shape=jax.ShapeDtypeStruct((2, m, cols), F32),
        in_specs=[vmem] * 4,
        out_specs=hbm,
        scratch_shapes=[pltpu.VMEM((2, m, cols), F32), pltpu.SemaphoreType.DMA((6,))],
        compiler_params=pltpu.CompilerParams(vmem_limit_bytes=32 * 1024 * 1024),
        name="finish",
    )(*outs)


def solution(mesh):
    split = Mesh(mesh.devices.reshape([SIZES[a] for a in AXES]), AXES)
    row, mode = ("zl", "y"), ("zh", "x", "c")
    placed = (P(None, row, mode), P(None, mode + row, None), P(row, None))
    return jax.shard_map(
        body, mesh=split, in_specs=placed, out_specs=P(None, row, mode), check_vma=False
    )
```

```python
import jax
import jax.numpy as jnp
from jax import lax
from jax.experimental import pallas as pl
from jax.experimental.pallas import tpu as pltpu
from jax.sharding import Mesh
from jax.sharding import PartitionSpec as P

AXES = ("zl", "y", "zh", "x", "c")
SIZES = {"zl": 4, "y": 4, "zh": 4, "x": 4, "c": 2}
CHUNKS = ((0, 128), (128, 64), (192, 64))
FIRST_ROWS = 48
BY_MESH = pl.DeviceIdType.MESH
XC = ((2, 0), (2, 1), (1, 0), (3, 0), (1, 1), (3, 1), (0, 1))
F32, BF16 = jnp.float32, jnp.bfloat16


def shifted(axis, by):
    return lax.rem(lax.axis_index(axis) + by, SIZES[axis])


def along_z(by):
    z = lax.rem(lax.axis_index("zh") * 4 + lax.axis_index("zl") + (by + 16), 16)
    return {"zh": lax.div(z, 4), "zl": lax.rem(z, 4)}


def partner(index, j):
    if j == 0:
        return index
    if j == 1:
        return index + 1 - 2 * lax.rem(index, 2)
    if j == 2:
        return lax.rem(index + 2, 4)
    return 3 - index


def halves(value):
    high = value.astype(BF16)
    return high, (value - high.astype(F32)).astype(BF16)


def dot(a, b, contract_b):
    dims = (((1,), (contract_b,)), ((), ()))
    return lax.dot_general(a, b, dims, preferred_element_type=F32)


def fields_dot(a_high, a_low, high, low):
    width = high.shape[1]
    if width < 256:
        both = dot(a_high, jnp.concatenate([high, low], axis=1), 0)
        main, cross = both[:, :width], both[:, width:]
    else:
        main, cross = dot(a_high, high, 0), dot(a_high, low, 0)
    return main + (cross + dot(a_low, high, 0))


def gradient_dot(a_high, a_low, high, low):
    if high.shape[1] < 256:
        main = dot(
            jnp.concatenate([a_high, a_low], axis=1), jnp.concatenate([high, high], axis=1), 1
        )
    else:
        main = dot(a_high, high, 1) + dot(a_low, high, 1)
    return main + dot(a_high, low, 1)


def swapped(value, signs):
    width = value.shape[1] // 2
    if width % 128 == 0:
        turned = jnp.concatenate([value[:, width:], value[:, :width]], axis=1)
    else:
        turned = pltpu.roll(value, width, 1)
    return turned * signs


def sign_row(width, first, second):
    lane = lax.broadcasted_iota(jnp.int32, (1, 2 * width), 1)
    return jnp.where(lane < width, F32(first), F32(second))


def stacked_residual(value):
    turned = swapped(value, sign_row(value.shape[1] // 2, 1, -1))
    return halves(jnp.concatenate([value, turned], axis=0))


def gather_kernel(u_hbm, s_hbm, i_hbm, *rest):
    n = len(CHUNKS)
    grad, res_out, last_h, last_l = rest[:4]
    uf, uh, ul, s_ref, i_ref, sh0, sl0, sh1, sl1, in_sems, out_sems, near, b_sems = rest[4:17]
    per = [rest[17 + 12 * k : 17 + 12 * (k + 1)] for k in range(n)]
    zl, y, x, c = (lax.axis_index(a) for a in ("zl", "y", "x", "c"))
    own = x * 2 + c
    up, down = shifted("y", 1), shifted("y", 3)
    rows = i_ref.shape[0]
    own_rows = pl.ds(pl.multiple_of(own * rows, 8), rows)

    s_copy = pltpu.make_async_copy(s_hbm, s_ref, in_sems.at[0])
    i_copy = pltpu.make_async_copy(i_hbm.at[own_rows, :], i_ref, in_sems.at[1])
    u_copy = pltpu.make_async_copy(u_hbm, uf, in_sems.at[2])
    s_copy.start()
    i_copy.start()
    u_copy.start()

    barrier = pltpu.get_barrier_semaphore()
    beside = [{"x": shifted("x", 1)}, {"x": shifted("x", 3)}]
    twin = {"c": 1 - c}
    peers = [{"zl": partner(zl, j)} for j in (1, 2, 3)]
    peers += [{"y": up}, {"y": down}, along_z(1), along_z(-1), twin] + beside
    for peer in peers:
        pl.semaphore_signal(barrier, inc=1, device_id=peer, device_id_type=BY_MESH)

    s_copy.wait()
    i_copy.wait()
    for k, (first, width) in enumerate(CHUNKS):
        strip = per[k][0]
        packed = jnp.concatenate(
            [s_ref[0, :, first : first + width], s_ref[1, :, first : first + width]], axis=1
        )
        strip[zl * 4 + y] = packed
        mine = i_ref[:, first : first + width]
        per[k][5][...] = jnp.concatenate([mine, mine], axis=1)

    pl.semaphore_wait(barrier, len(peers))

    def announce(i):
        for by in (1 << i, -(1 << i)):
            pl.semaphore_signal(near.at[i], inc=1, device_id=along_z(by), device_id_type=BY_MESH)

    def heard(i):
        pl.semaphore_wait(near.at[i], 2)

    def announce_x(i):
        for peer in beside + [twin][i:]:
            pl.semaphore_signal(near.at[3 + i], inc=1, device_id=peer, device_id_type=BY_MESH)

    def heard_x(i):
        pl.semaphore_wait(near.at[3 + i], 3 - i)

    announce(0)
    announce_x(0)

    def send(src, dst, send_sem, recv_sem, peer):
        pltpu.make_async_remote_copy(
            src_ref=src, dst_ref=dst, send_sem=send_sem, recv_sem=recv_sem,
            device_id=peer, device_id_type=BY_MESH,
        ).start()

    def await_bytes(of, sem):
        pltpu.make_async_copy(of, of, sem).wait()

    def place(j, at):
        return partner(zl, j) * 4 + at

    def leading(k):
        return per[k][0].shape[1] if k < n - 1 else FIRST_ROWS

    trailing = pl.ds(FIRST_ROWS, per[n - 1][0].shape[1] - FIRST_ROWS)

    def part(k, at):
        return per[k][0].at[at, pl.ds(0, leading(k))]

    def part_half(k, at, h):
        size = leading(k) // 2
        return per[k][0].at[at, pl.ds(size * h, size)]

    def parts_like(k, count):
        return per[k][0].at[pl.ds(0, count), pl.ds(0, leading(k))]

    def both_ways(k, j):
        sem, arrived = per[k][6], per[k][8].at[j]
        block = part(k, place(j, y))
        send(block, block, sem, arrived, {"y": up})
        send(block, block, sem, arrived, {"y": down})
        if direct(k, j):
            send(block, block, sem, per[k][9].at[j], {"y": shifted("y", 2)})

    def direct(k, j):
        return j > (3, 2, 0)[k]

    def issue(k):
        sem, arrived = per[k][6], per[k][7]
        block = part(k, place(0, y))
        for j in (1, 2, 3):
            send(block, block, sem, arrived.at[j - 1], {"zl": partner(zl, j)})
        both_ways(k, 0)
        if k == n - 1:
            turn(up)
            turn(down)

    def turn(to):
        block = per[n - 1][0].at[place(0, y), trailing]
        send(block, block, per[n - 1][6], b_sems.at[0], {"y": to})

    def cross():
        strip, sem = per[n - 1][0], per[n - 1][6]
        await_bytes(strip.at[pl.ds(0, 3), trailing], b_sems.at[0])
        column = strip.at[pl.ds(zl * 4, 4), trailing]
        for j in (1, 2, 3):
            send(column, column, sem, b_sems.at[j], {"zl": partner(zl, j)})

    def relay(k, j):
        sem, arrived = per[k][6], per[k][9].at[j]
        await_bytes(parts_like(k, 2), per[k][8].at[j])
        if not direct(k, j):
            from_down = part_half(k, place(j, down), 0)
            from_up = part_half(k, place(j, up), 1)
            send(from_down, from_down, sem, arrived, {"y": up})
            send(from_up, from_up, sem, arrived, {"y": down})

    def forward(k, j):
        await_bytes(part(k, 0), per[k][7].at[j - 1])
        both_ways(k, j)

    def relay_rest(k):
        for j in (1, 2, 3):
            relay(k, j)

    def forward_all(k):
        for j in (1, 2, 3):
            forward(k, j)

    def gather_first():
        for j in (0, 1, 2, 3):
            if j < 3:
                forward(0, j + 1)
            if j < 3:
                heard(j)
            if j < 2:
                announce(j + 1)
            if j == 2:
                cross()
            relay(0, j)
            if j == 0:
                turn(shifted("y", 2))
            if j < 2:
                relay(j + 1, 0)
                heard_x(j)
            if j == 0:
                announce_x(1)

    def fields(k, t):
        strip, total = per[k][:2]
        width = CHUNKS[k][1]
        keep_high, keep_low = kept(k)
        for j in (2 * t, 2 * t + 1):
            await_bytes(part(k, 0), per[k][9].at[j])
            if k == n - 1 and j > 0:
                await_bytes(strip.at[pl.ds(0, 4), trailing], b_sems.at[j])
        q = lax.div(zl, 2) if t == 0 else 1 - lax.div(zl, 2)
        high, low = halves(strip[pl.ds(q * 8, 8)].reshape(768, 2 * width))
        keep_high[q] = high
        keep_low[q] = low
        value = fields_dot(uh[q], ul[q], high, low)
        if t == 0:
            total[...] = value
        else:
            total[...] += value

    def spread_fields(k):
        total, parts, got = per[k][1:4]
        width = CHUNKS[k][1]
        half = total.shape[0] // 2
        value = total[:half, :] + swapped(total[half:, :], sign_row(width, -1, 1))
        parts[...] = value.reshape(parts.shape)
        for i, (dx, dc) in enumerate(XC):
            tx, tc = shifted("x", dx), shifted("c", dc)
            part = parts.at[tx * 2 + tc]
            send(part, got.at[i], per[k][10].at[0], per[k][11].at[0], {"x": tx, "c": tc})

    def sum_over_x(k):
        parts, got, share = per[k][2], per[k][3], per[k][4]
        await_bytes(got, per[k][11].at[0])
        value = parts[own]
        for i in range(7):
            value = value + got[i]
        share[0] = value
        for d in (2, 1, 3):
            peer = {"zh": shifted("zh", d)}
            send(share.at[0], share.at[d], per[k][10].at[1], per[k][11].at[1], peer)

    def spread_residual(k):
        share, measured = per[k][4], per[k][5]
        await_bytes(share.at[pl.ds(1, 3)], per[k][11].at[1])
        value = (share[0] + share[1]) + (share[2] + share[3])
        square = value * value
        excess = square + swapped(square, F32(1)) - measured[...]
        share[4] = excess * value * F32(1 / 256)
        mine = gathered(k).at[own_rows, :]
        for dx, dc in XC:
            peer = {"x": shifted("x", dx), "c": shifted("c", dc)}
            send(share.at[4], mine, per[k][10].at[2], per[k][11].at[2], peer)
        pltpu.make_async_copy(share.at[4], mine, out_sems.at[k]).start()

    def kept(k):
        return ((sh0, sl0), (sh1, sl1), (last_h, last_l))[k]

    def gathered(k):
        return per[k][1].at[: 8 * rows, :] if k < n - 1 else res_out

    def await_residual(k):
        await_bytes(per[k][3], per[k][11].at[2])
        await_bytes(per[k][4].at[4], out_sems.at[k])

    def gradient(k):
        await_residual(k)
        high, low = stacked_residual(per[k][1][: 8 * rows, :])
        keep_high, keep_low = kept(k)
        for q in range(2):
            value = gradient_dot(high, low, keep_high[q], keep_low[q]).reshape(2, 8 * rows, 768)
            if k == 0:
                grad[:, :, q * 768 : (q + 1) * 768] = value
            else:
                grad[:, :, q * 768 : (q + 1) * 768] += value

    def drain(k):
        await_bytes(per[k][0].at[pl.ds(0, 15)], per[k][6])
        await_bytes(per[k][3], per[k][10].at[0])
        await_bytes(per[k][4].at[pl.ds(0, 3)], per[k][10].at[1])
        await_bytes(per[k][3], per[k][10].at[2])

    for k in range(n):
        issue(k)

    u_copy.wait()
    for q in range(2):
        for p in range(2):
            high, low = halves(uf[p, :, q * 768 : (q + 1) * 768])
            uh[q, p * 192 : (p + 1) * 192, :] = high
            ul[q, p * 192 : (p + 1) * 192, :] = low

    gather_first()
    forward_all(1)
    fields(0, 0)
    fields(0, 1)
    spread_fields(0)
    relay_rest(1)
    forward_all(2)
    fields(1, 0)
    fields(1, 1)
    spread_fields(1)
    relay_rest(2)
    sum_over_x(0)
    fields(2, 0)
    fields(2, 1)
    spread_fields(2)
    sum_over_x(1)
    sum_over_x(2)
    spread_residual(0)
    spread_residual(1)
    spread_residual(2)
    gradient(0)
    gradient(1)
    for k in range(n):
        drain(k)
    await_residual(2)


def finish_kernel(grad, res, last_h, last_l, out, done, sems):
    high, low = stacked_residual(res[...])
    copies = []
    for g in range(6):
        of = (g // 3, pl.ds(g % 3 * 256, 256))
        value = gradient_dot(high, low, last_h[of], last_l[of])
        columns = pl.ds(g * 256, 256)
        done[:, :, columns] = grad[:, :, columns] + value.reshape(2, value.shape[0] // 2, 256)
        copy = pltpu.make_async_copy(done.at[:, :, columns], out.at[:, :, columns], sems.at[g])
        copy.start()
        copies.append(copy)
    for copy in copies:
        copy.wait()


def body(transfer_matrix, probes, intensity):
    _, m, cols = transfer_matrix.shape
    rows = m // 8
    width = CHUNKS[-1][1]
    vmem = pl.BlockSpec(memory_space=pltpu.VMEM)
    hbm = pl.BlockSpec(memory_space=pltpu.HBM)
    scratch = [
        pltpu.VMEM((2, m, cols), F32),
        pltpu.VMEM((2, 2 * m, cols // 2), BF16),
        pltpu.VMEM((2, 2 * m, cols // 2), BF16),
        pltpu.VMEM(probes.shape, F32),
        pltpu.VMEM((rows, intensity.shape[1]), F32),
        pltpu.VMEM((2, cols // 2, 2 * CHUNKS[0][1]), BF16),
        pltpu.VMEM((2, cols // 2, 2 * CHUNKS[0][1]), BF16),
        pltpu.VMEM((2, cols // 2, 2 * CHUNKS[1][1]), BF16),
        pltpu.VMEM((2, cols // 2, 2 * CHUNKS[1][1]), BF16),
        pltpu.SemaphoreType.DMA((3,)),
        pltpu.SemaphoreType.DMA((3,)),
        pltpu.SemaphoreType.REGULAR((5,)),
        pltpu.SemaphoreType.DMA((4,)),
    ]
    for _, w in CHUNKS:
        scratch += [
            pltpu.VMEM((16, cols // 16, 2 * w), F32),
            pltpu.VMEM((2 * m, 2 * w), F32),
            pltpu.VMEM((8, rows, 2 * w), F32),
            pltpu.VMEM((7, rows, 2 * w), F32),
            pltpu.VMEM((5, rows, 2 * w), F32),
            pltpu.VMEM((rows, 2 * w), F32),
            pltpu.SemaphoreType.DMA,
            pltpu.SemaphoreType.DMA((3,)),
            pltpu.SemaphoreType.DMA((4,)),
            pltpu.SemaphoreType.DMA((4,)),
            pltpu.SemaphoreType.DMA((3,)),
            pltpu.SemaphoreType.DMA((3,)),
        ]
    outs = pl.pallas_call(
        gather_kernel,
        out_shape=(
            jax.ShapeDtypeStruct((2, m, cols), F32),
            jax.ShapeDtypeStruct((m, 2 * width), F32),
            jax.ShapeDtypeStruct((2, cols // 2, 2 * width), BF16),
            jax.ShapeDtypeStruct((2, cols // 2, 2 * width), BF16),
        ),
        in_specs=[hbm] * 3,
        out_specs=(vmem,) * 4,
        scratch_shapes=scratch,
        compiler_params=pltpu.CompilerParams(
            collective_id=0, has_side_effects=True, vmem_limit_bytes=32 * 1024 * 1024
        ),
        name="gather",
    )(*(pltpu.with_memory_space_constraint(a, pltpu.HBM) for a in (transfer_matrix, probes, intensity)))
    return pl.pallas_call(
        finish_kernel,
        out_shape=jax.ShapeDtypeStruct((2, m, cols), F32),
        in_specs=[vmem] * 4,
        out_specs=hbm,
        scratch_shapes=[pltpu.VMEM((2, m, cols), F32), pltpu.SemaphoreType.DMA((6,))],
        compiler_params=pltpu.CompilerParams(vmem_limit_bytes=32 * 1024 * 1024),
        name="finish",
    )(*outs)


def solution(mesh):
    split = Mesh(mesh.devices.reshape([SIZES[a] for a in AXES]), AXES)
    row, mode = ("zl", "y"), ("zh", "x", "c")
    placed = (P(None, row, mode), P(None, mode + row, None), P(row, None))
    return jax.shard_map(
        body, mesh=split, in_specs=placed, out_specs=P(None, row, mode), check_vma=False
    )
```

```python
import jax
import jax.numpy as jnp
from jax import lax
from jax.experimental import pallas as pl
from jax.experimental.pallas import tpu as pltpu
from jax.sharding import Mesh
from jax.sharding import PartitionSpec as P

AXES = ("zl", "y", "zh", "x", "c")
SIZES = {"zl": 4, "y": 4, "zh": 4, "x": 4, "c": 2}
CHUNKS = ((0, 128), (128, 64), (192, 64))
FIRST_ROWS = 48
BY_MESH = pl.DeviceIdType.MESH
XC = ((2, 0), (2, 1), (1, 0), (3, 0), (1, 1), (3, 1), (0, 1))
F32, BF16 = jnp.float32, jnp.bfloat16


def shifted(axis, by):
    return lax.rem(lax.axis_index(axis) + by, SIZES[axis])


def along_z(by):
    z = lax.rem(lax.axis_index("zh") * 4 + lax.axis_index("zl") + (by + 16), 16)
    return {"zh": lax.div(z, 4), "zl": lax.rem(z, 4)}


def partner(index, j):
    if j == 0:
        return index
    if j == 1:
        return index + 1 - 2 * lax.rem(index, 2)
    if j == 2:
        return lax.rem(index + 2, 4)
    return 3 - index


def halves(value):
    high = value.astype(BF16)
    return high, (value - high.astype(F32)).astype(BF16)


def dot(a, b, contract_b):
    dims = (((1,), (contract_b,)), ((), ()))
    return lax.dot_general(a, b, dims, preferred_element_type=F32)


def fields_dot(a_high, a_low, high, low):
    width = high.shape[1]
    if width < 256:
        both = dot(a_high, jnp.concatenate([high, low], axis=1), 0)
        main, cross = both[:, :width], both[:, width:]
    else:
        main, cross = dot(a_high, high, 0), dot(a_high, low, 0)
    return main + (cross + dot(a_low, high, 0))


def gradient_dot(a_high, a_low, high, low):
    if high.shape[1] < 256:
        main = dot(
            jnp.concatenate([a_high, a_low], axis=1), jnp.concatenate([high, high], axis=1), 1
        )
    else:
        main = dot(a_high, high, 1) + dot(a_low, high, 1)
    return main + dot(a_high, low, 1)


def swapped(value, signs):
    width = value.shape[1] // 2
    if width % 128 == 0:
        turned = jnp.concatenate([value[:, width:], value[:, :width]], axis=1)
    else:
        turned = pltpu.roll(value, width, 1)
    return turned * signs


def sign_row(width, first, second):
    lane = lax.broadcasted_iota(jnp.int32, (1, 2 * width), 1)
    return jnp.where(lane < width, F32(first), F32(second))


def stacked_residual(value):
    turned = swapped(value, sign_row(value.shape[1] // 2, 1, -1))
    return halves(jnp.concatenate([value, turned], axis=0))


def gather_kernel(u_hbm, s_hbm, i_hbm, *rest):
    n = len(CHUNKS)
    grad, res_out, last_h, last_l = rest[:4]
    uf, uh, ul, s_ref, i_ref, sh0, sl0, sh1, sl1, in_sems, out_sems, near, b_sems = rest[4:17]
    per = [rest[17 + 12 * k : 17 + 12 * (k + 1)] for k in range(n)]
    zl, y, x, c = (lax.axis_index(a) for a in ("zl", "y", "x", "c"))
    own = x * 2 + c
    up, down = shifted("y", 1), shifted("y", 3)
    rows = i_ref.shape[0]
    own_rows = pl.ds(pl.multiple_of(own * rows, 8), rows)

    s_copy = pltpu.make_async_copy(s_hbm, s_ref, in_sems.at[0])
    i_copy = pltpu.make_async_copy(i_hbm.at[own_rows, :], i_ref, in_sems.at[1])
    u_copy = pltpu.make_async_copy(u_hbm, uf, in_sems.at[2])
    s_copy.start()
    i_copy.start()
    u_copy.start()

    barrier = pltpu.get_barrier_semaphore()
    beside = [{"x": shifted("x", 1)}, {"x": shifted("x", 3)}]
    twin = {"c": 1 - c}
    peers = [{"zl": partner(zl, j)} for j in (1, 2, 3)]
    peers += [{"y": up}, {"y": down}, along_z(1), along_z(-1), twin] + beside
    for peer in peers:
        pl.semaphore_signal(barrier, inc=1, device_id=peer, device_id_type=BY_MESH)

    s_copy.wait()
    i_copy.wait()
    for k, (first, width) in enumerate(CHUNKS):
        strip = per[k][0]
        packed = jnp.concatenate(
            [s_ref[0, :, first : first + width], s_ref[1, :, first : first + width]], axis=1
        )
        strip[zl * 4 + y] = packed
        mine = i_ref[:, first : first + width]
        per[k][5][...] = jnp.concatenate([mine, mine], axis=1)

    pl.semaphore_wait(barrier, len(peers))

    def announce(i):
        for by in (1 << i, -(1 << i)):
            pl.semaphore_signal(near.at[i], inc=1, device_id=along_z(by), device_id_type=BY_MESH)

    def heard(i):
        pl.semaphore_wait(near.at[i], 2)

    def announce_x(i):
        for peer in beside + [twin][i:]:
            pl.semaphore_signal(near.at[3 + i], inc=1, device_id=peer, device_id_type=BY_MESH)

    def heard_x(i):
        pl.semaphore_wait(near.at[3 + i], 3 - i)

    announce(0)
    announce_x(0)

    def send(src, dst, send_sem, recv_sem, peer):
        pltpu.make_async_remote_copy(
            src_ref=src, dst_ref=dst, send_sem=send_sem, recv_sem=recv_sem,
            device_id=peer, device_id_type=BY_MESH,
        ).start()

    def await_bytes(of, sem):
        pltpu.make_async_copy(of, of, sem).wait()

    def place(j, at):
        return partner(zl, j) * 4 + at

    def leading(k):
        return per[k][0].shape[1] if k < n - 1 else FIRST_ROWS

    trailing = pl.ds(FIRST_ROWS, per[n - 1][0].shape[1] - FIRST_ROWS)

    def part(k, at):
        return per[k][0].at[at, pl.ds(0, leading(k))]

    def part_half(k, at, h):
        size = leading(k) // 2
        return per[k][0].at[at, pl.ds(size * h, size)]

    def parts_like(k, count):
        return per[k][0].at[pl.ds(0, count), pl.ds(0, leading(k))]

    def both_ways(k, j):
        sem, arrived = per[k][6], per[k][8].at[j]
        block = part(k, place(j, y))
        if direct(k, j):
            send(block, block, sem, per[k][9].at[j], {"y": shifted("y", 2)})
        send(block, block, sem, arrived, {"y": up})
        send(block, block, sem, arrived, {"y": down})

    def direct(k, j):
        return j > (3, 2, 0)[k]

    def issue(k):
        sem, arrived = per[k][6], per[k][7]
        block = part(k, place(0, y))
        for j in (1, 2, 3):
            send(block, block, sem, arrived.at[j - 1], {"zl": partner(zl, j)})
        both_ways(k, 0)
        if k == n - 1:
            turn(up)
            turn(down)

    def turn(to):
        block = per[n - 1][0].at[place(0, y), trailing]
        send(block, block, per[n - 1][6], b_sems.at[0], {"y": to})

    def cross():
        strip, sem = per[n - 1][0], per[n - 1][6]
        await_bytes(strip.at[pl.ds(0, 3), trailing], b_sems.at[0])
        column = strip.at[pl.ds(zl * 4, 4), trailing]
        for j in (1, 2, 3):
            send(column, column, sem, b_sems.at[j], {"zl": partner(zl, j)})

    def relay(k, j):
        sem, arrived = per[k][6], per[k][9].at[j]
        await_bytes(parts_like(k, 2), per[k][8].at[j])
        if not direct(k, j):
            from_down = part_half(k, place(j, down), 0)
            from_up = part_half(k, place(j, up), 1)
            send(from_down, from_down, sem, arrived, {"y": up})
            send(from_up, from_up, sem, arrived, {"y": down})

    def forward(k, j):
        await_bytes(part(k, 0), per[k][7].at[j - 1])
        both_ways(k, j)

    def relay_rest(k):
        for j in (1, 2, 3):
            relay(k, j)

    def forward_all(k):
        for j in (1, 2, 3):
            forward(k, j)

    def gather_first():
        for j in (0, 1, 2, 3):
            if j < 3:
                forward(0, j + 1)
            if j < 3:
                heard(j)
            if j < 2:
                announce(j + 1)
            if j == 2:
                cross()
            relay(0, j)
            if j == 0:
                turn(shifted("y", 2))
            if j < 2:
                relay(j + 1, 0)
                heard_x(j)
            if j == 0:
                announce_x(1)

    def fields(k, t):
        strip, total = per[k][:2]
        width = CHUNKS[k][1]
        keep_high, keep_low = kept(k)
        for j in (2 * t, 2 * t + 1):
            await_bytes(part(k, 0), per[k][9].at[j])
            if k == n - 1 and j > 0:
                await_bytes(strip.at[pl.ds(0, 4), trailing], b_sems.at[j])
        q = lax.div(zl, 2) if t == 0 else 1 - lax.div(zl, 2)
        high, low = halves(strip[pl.ds(q * 8, 8)].reshape(768, 2 * width))
        keep_high[q] = high
        keep_low[q] = low
        value = fields_dot(uh[q], ul[q], high, low)
        if t == 0:
            total[...] = value
        else:
            total[...] += value

    def spread_fields(k):
        total, parts, got = per[k][1:4]
        width = CHUNKS[k][1]
        half = total.shape[0] // 2
        value = total[:half, :] + swapped(total[half:, :], sign_row(width, -1, 1))
        parts[...] = value.reshape(parts.shape)
        for i, (dx, dc) in enumerate(XC):
            tx, tc = shifted("x", dx), shifted("c", dc)
            part = parts.at[tx * 2 + tc]
            send(part, got.at[i], per[k][10].at[0], per[k][11].at[0], {"x": tx, "c": tc})

    def sum_over_x(k):
        parts, got, share = per[k][2], per[k][3], per[k][4]
        await_bytes(got, per[k][11].at[0])
        value = parts[own]
        for i in range(7):
            value = value + got[i]
        share[0] = value
        for d in (2, 1, 3):
            peer = {"zh": shifted("zh", d)}
            send(share.at[0], share.at[d], per[k][10].at[1], per[k][11].at[1], peer)

    def spread_residual(k):
        share, measured = per[k][4], per[k][5]
        await_bytes(share.at[pl.ds(1, 3)], per[k][11].at[1])
        value = (share[0] + share[1]) + (share[2] + share[3])
        square = value * value
        excess = square + swapped(square, F32(1)) - measured[...]
        share[4] = excess * value * F32(1 / 256)
        mine = gathered(k).at[own_rows, :]
        for dx, dc in XC:
            peer = {"x": shifted("x", dx), "c": shifted("c", dc)}
            send(share.at[4], mine, per[k][10].at[2], per[k][11].at[2], peer)
        pltpu.make_async_copy(share.at[4], mine, out_sems.at[k]).start()

    def kept(k):
        return ((sh0, sl0), (sh1, sl1), (last_h, last_l))[k]

    def gathered(k):
        return per[k][1].at[: 8 * rows, :] if k < n - 1 else res_out

    def await_residual(k):
        await_bytes(per[k][3], per[k][11].at[2])
        await_bytes(per[k][4].at[4], out_sems.at[k])

    def gradient(k):
        await_residual(k)
        high, low = stacked_residual(per[k][1][: 8 * rows, :])
        keep_high, keep_low = kept(k)
        for q in range(2):
            value = gradient_dot(high, low, keep_high[q], keep_low[q]).reshape(2, 8 * rows, 768)
            if k == 0:
                grad[:, :, q * 768 : (q + 1) * 768] = value
            else:
                grad[:, :, q * 768 : (q + 1) * 768] += value

    def drain(k):
        await_bytes(per[k][0].at[pl.ds(0, 15)], per[k][6])
        await_bytes(per[k][3], per[k][10].at[0])
        await_bytes(per[k][4].at[pl.ds(0, 3)], per[k][10].at[1])
        await_bytes(per[k][3], per[k][10].at[2])

    for k in range(n):
        issue(k)

    u_copy.wait()
    for q in range(2):
        for p in range(2):
            high, low = halves(uf[p, :, q * 768 : (q + 1) * 768])
            uh[q, p * 192 : (p + 1) * 192, :] = high
            ul[q, p * 192 : (p + 1) * 192, :] = low

    gather_first()
    forward_all(1)
    fields(0, 0)
    fields(0, 1)
    spread_fields(0)
    relay_rest(1)
    forward_all(2)
    fields(1, 0)
    fields(1, 1)
    spread_fields(1)
    relay_rest(2)
    sum_over_x(0)
    fields(2, 0)
    fields(2, 1)
    spread_fields(2)
    sum_over_x(1)
    sum_over_x(2)
    spread_residual(0)
    spread_residual(1)
    spread_residual(2)
    gradient(0)
    gradient(1)
    for k in range(n):
        drain(k)
    await_residual(2)


def finish_kernel(grad, res, last_h, last_l, out, done, sems):
    high, low = stacked_residual(res[...])
    copies = []
    for g in range(6):
        of = (g // 3, pl.ds(g % 3 * 256, 256))
        value = gradient_dot(high, low, last_h[of], last_l[of])
        columns = pl.ds(g * 256, 256)
        done[:, :, columns] = grad[:, :, columns] + value.reshape(2, value.shape[0] // 2, 256)
        copy = pltpu.make_async_copy(done.at[:, :, columns], out.at[:, :, columns], sems.at[g])
        copy.start()
        copies.append(copy)
    for copy in copies:
        copy.wait()


def body(transfer_matrix, probes, intensity):
    _, m, cols = transfer_matrix.shape
    rows = m // 8
    width = CHUNKS[-1][1]
    vmem = pl.BlockSpec(memory_space=pltpu.VMEM)
    hbm = pl.BlockSpec(memory_space=pltpu.HBM)
    scratch = [
        pltpu.VMEM((2, m, cols), F32),
        pltpu.VMEM((2, 2 * m, cols // 2), BF16),
        pltpu.VMEM((2, 2 * m, cols // 2), BF16),
        pltpu.VMEM(probes.shape, F32),
        pltpu.VMEM((rows, intensity.shape[1]), F32),
        pltpu.VMEM((2, cols // 2, 2 * CHUNKS[0][1]), BF16),
        pltpu.VMEM((2, cols // 2, 2 * CHUNKS[0][1]), BF16),
        pltpu.VMEM((2, cols // 2, 2 * CHUNKS[1][1]), BF16),
        pltpu.VMEM((2, cols // 2, 2 * CHUNKS[1][1]), BF16),
        pltpu.SemaphoreType.DMA((3,)),
        pltpu.SemaphoreType.DMA((3,)),
        pltpu.SemaphoreType.REGULAR((5,)),
        pltpu.SemaphoreType.DMA((4,)),
    ]
    for _, w in CHUNKS:
        scratch += [
            pltpu.VMEM((16, cols // 16, 2 * w), F32),
            pltpu.VMEM((2 * m, 2 * w), F32),
            pltpu.VMEM((8, rows, 2 * w), F32),
            pltpu.VMEM((7, rows, 2 * w), F32),
            pltpu.VMEM((5, rows, 2 * w), F32),
            pltpu.VMEM((rows, 2 * w), F32),
            pltpu.SemaphoreType.DMA,
            pltpu.SemaphoreType.DMA((3,)),
            pltpu.SemaphoreType.DMA((4,)),
            pltpu.SemaphoreType.DMA((4,)),
            pltpu.SemaphoreType.DMA((3,)),
            pltpu.SemaphoreType.DMA((3,)),
        ]
    outs = pl.pallas_call(
        gather_kernel,
        out_shape=(
            jax.ShapeDtypeStruct((2, m, cols), F32),
            jax.ShapeDtypeStruct((m, 2 * width), F32),
            jax.ShapeDtypeStruct((2, cols // 2, 2 * width), BF16),
            jax.ShapeDtypeStruct((2, cols // 2, 2 * width), BF16),
        ),
        in_specs=[hbm] * 3,
        out_specs=(vmem,) * 4,
        scratch_shapes=scratch,
        compiler_params=pltpu.CompilerParams(
            collective_id=0, has_side_effects=True, vmem_limit_bytes=32 * 1024 * 1024
        ),
        name="gather",
    )(*(pltpu.with_memory_space_constraint(a, pltpu.HBM) for a in (transfer_matrix, probes, intensity)))
    return pl.pallas_call(
        finish_kernel,
        out_shape=jax.ShapeDtypeStruct((2, m, cols), F32),
        in_specs=[vmem] * 4,
        out_specs=hbm,
        scratch_shapes=[pltpu.VMEM((2, m, cols), F32), pltpu.SemaphoreType.DMA((6,))],
        compiler_params=pltpu.CompilerParams(vmem_limit_bytes=32 * 1024 * 1024),
        name="finish",
    )(*outs)


def solution(mesh):
    split = Mesh(mesh.devices.reshape([SIZES[a] for a in AXES]), AXES)
    row, mode = ("zl", "y"), ("zh", "x", "c")
    placed = (P(None, row, mode), P(None, mode + row, None), P(row, None))
    return jax.shard_map(
        body, mesh=split, in_specs=placed, out_specs=P(None, row, mode), check_vma=False
    )
```
